32 devices in a mesh: grp: 2 (over x), tm: 8 (over z, y), blk: 2 (over core).
Axes of the slice: x: 2, y: 2, z: 4, core: 2. Of those that a mesh axis runs over, the one named last changes fastest.
Arguments:
- hyper_params: float32 [6], P('grp'), parts along dimension 0, as said below
- space_precision: float32 [256, 256], P('blk'), may hold values from -1 to 16, as said below
- data_precision: float32 [32, 256, 256], P(('grp', 'tm'), 'blk'), parts along dimension 0, may hold values from -1 to 4, as said below
- covariates: float32 [32, 32, 256], P(('grp', 'tm'), None, 'blk'), parts along dimension 0
- fixed_precision: float32 [64], P('grp'), parts along dimension 0, may hold values from 0.5 to 2
Outputs:
- day_covariance: float32 [32, 256, 256], P(('grp', 'tm'), 'blk'), parts along dimension 0
- day_gradients: float32 [3, 32], P(None, ('grp', 'tm')), parts along dimension 1
- fixed_covariance: float32 [64, 32], P('grp'), parts along dimension 0
The draws below stay inside these ranges and needn't reach their ends.
There are 2 independent parts, one for each index of `grp`. The reference program is written for one: setup_inputs(seed, part) draws one part's arguments, and reference() takes and returns one part's arrays. A program takes and returns all parts, laid end to end along the dimension named above; an argument that names none is the same for every part. Nothing has to cross between parts.
Inputs may be any that keep to these rules, and one draw needn't show every extreme that they name: `hyper_params`: entries 0 and 2 lie in -0.3 to 0.3; entry 1 equals atanh(1 - e) with e between 1.5 / 16 and 6 / 16. `space_precision`: symmetric positive definite. `data_precision`: each day's block is symmetric positive definite.
All inputs are finite; a program needn't handle non-finite values.
Results may differ from the reference program's by a relative error of at most 0.0003.
Values sent between devices are 32-bit elements; how exact they have to be, the bound alone decides.
A program may use at most 128 MiB of HBM per device.

```python
import math
import jax
import jax.numpy as jnp
from jax import lax

NODES = 256
FIXED = 32
DAYS = 16


def symmetric_blocks(key, count_blocks, extent):
    keys = jax.random.split(key, 2)
    raw_values = jax.random.uniform(keys[0], (count_blocks, extent, extent), jnp.float32, -1.0, 1.0)
    mixed = (raw_values + jnp.swapaxes(raw_values, 1, 2)) * (0.5 * 1.35 / math.sqrt(extent))
    uniform_part = jax.random.uniform(keys[1], (count_blocks, extent), jnp.float32)
    diagonal = 1.6 + 2.0 * uniform_part
    identity = jnp.eye(extent, dtype=jnp.float32)
    return mixed * (1.0 - identity) + diagonal[:, :, None] * identity


def draw_hyper_params(key, part):
    uniform_part = jax.random.uniform(jax.random.fold_in(key, 14), (3,), jnp.float32)
    edge_value = (3.0 + 3.0 * uniform_part[1]) / DAYS
    middle = 0.5 * jnp.log((2.0 - edge_value) / edge_value)
    others = -0.3 + 0.6 * uniform_part
    return jnp.stack([others[0], middle, others[2]])


def draw_space_precision(key, part):
    return 4.0 * symmetric_blocks(jax.random.fold_in(key, 11), 1, NODES)[0]


def draw_data_precision(key, part):
    level_value = 64.0 / (DAYS * DAYS)
    blocks = symmetric_blocks(jax.random.fold_in(key, 12), DAYS, NODES) * level_value
    return blocks


def draw_covariates(key, part):
    base = jax.random.normal(jax.random.fold_in(key, 13), (DAYS, FIXED, NODES), jnp.float32)
    rising = 1.0 + 2.0 * jnp.arange(DAYS, dtype=jnp.float32) / max(DAYS - 1, 1)
    scale_value = 0.0625 * math.sqrt(DAYS / NODES)
    return base * scale_value * rising[:, None, None]


def setup_inputs(seed: int = 0, part: int = 0) -> dict:
    key_of = jax.random.split(jax.random.key(seed), 6)
    part_keys = jax.random.split(jax.random.fold_in(key_of[5], part), 6)
    hyper_params = draw_hyper_params(jax.random.fold_in(jax.random.fold_in(key_of[5], part), 71), part)
    space_precision = draw_space_precision(jax.random.fold_in(key_of[5], 71), part)
    data_precision = draw_data_precision(jax.random.fold_in(jax.random.fold_in(key_of[5], part), 71), part)
    covariates = draw_covariates(jax.random.fold_in(jax.random.fold_in(key_of[5], part), 71), part)
    fixed_precision = jnp.clip(jnp.exp(jax.random.uniform(part_keys[4], (FIXED,), jnp.float32, math.log(0.5), math.log(2.0))), 0.5, 2.0)
    return dict(hyper_params=hyper_params, space_precision=space_precision, data_precision=data_precision, covariates=covariates, fixed_precision=fixed_precision)


HIGHEST = lax.Precision.HIGHEST

def product(multiplier, multiplicand):
    return jnp.dot(multiplier.astype(jnp.float32), multiplicand.astype(jnp.float32), precision=HIGHEST, preferred_element_type=jnp.float32)

def frobenius(matrix_one, matrix_two):
    return jnp.sum(matrix_one * matrix_two)

def inverse_full(matrix):
    factor = jnp.linalg.cholesky(matrix)
    identity = jnp.eye(matrix.shape[0], dtype=matrix.dtype)
    return jax.scipy.linalg.cho_solve((factor, True), identity)

def reference(hyper_params, space_precision, data_precision, covariates, fixed_precision):
    prior_scale = jnp.exp(hyper_params[0])
    correlation = jnp.tanh(hyper_params[1])
    noise_scale = jnp.exp(hyper_params[2])
    complement = 1.0 - correlation * correlation
    day_index = jnp.arange(DAYS)
    border = (day_index == 0) | (day_index == DAYS - 1)
    weight = jnp.where(border, 1.0, 1.0 + correlation * correlation)
    weight_rate = jnp.where(border, 0.0, 2.0 * correlation * complement)
    couple = -prior_scale * correlation * space_precision
    arrow_blocks = noise_scale * jnp.einsum('dfi,dij->dfj', covariates, data_precision, precision=HIGHEST)
    data_gram = jnp.einsum('dfj,dgj->fg', arrow_blocks, covariates, precision=HIGHEST)

    def forward(carried, inputs):
        pending_block, pending_side, schur_terms = carried
        observed_day, arrow_day, weight_day = inputs
        square = prior_scale * weight_day * space_precision + noise_scale * observed_day + pending_block
        side_link = arrow_day + pending_side
        inverse = inverse_full(square)
        side_inverse = product(side_link, inverse)
        next_block = -product(product(couple, inverse), couple.T)
        next_side = -product(side_inverse, couple.T)
        schur_terms = schur_terms - product(side_inverse, side_link.T)
        return ((next_block, next_side, schur_terms), (inverse, side_link))
    start_state = (jnp.zeros((NODES, NODES), space_precision.dtype), jnp.zeros((FIXED, NODES), space_precision.dtype), jnp.zeros((FIXED, FIXED), space_precision.dtype))
    final_state, saved = lax.scan(forward, start_state, (data_precision, arrow_blocks, weight))
    inverses, side_links = saved
    schur_matrix = jnp.diag(fixed_precision) + data_gram + final_state[2]
    fixed_sigma = inverse_full(schur_matrix)

    def backward(carried, inputs):
        next_self, next_side = carried
        inverse, side_link, observed_day, arrow_day = inputs
        cross = -product(inverse, product(couple.T, next_self) + product(side_link.T, next_side))
        side_sigma = -product(product(next_side, couple) + product(fixed_sigma, side_link), inverse)
        self_sigma = inverse - product(product(cross, couple) + product(side_sigma.T, side_link), inverse)
        stats = jnp.stack([frobenius(self_sigma, space_precision), frobenius(self_sigma, observed_day), frobenius(side_sigma, arrow_day), frobenius(cross.T, space_precision)])
        return ((self_sigma, side_sigma), (self_sigma, stats))
    back_start = (jnp.zeros((NODES, NODES), space_precision.dtype), jnp.zeros((FIXED, NODES), space_precision.dtype))
    back_state, outputs = lax.scan(backward, back_start, (inverses, side_links, data_precision, arrow_blocks), reverse=True)
    day_sigma, stats = outputs
    trace_space = stats[:, 0]
    trace_data = stats[:, 1]
    trace_side = stats[:, 2]
    trace_cross = jnp.concatenate([jnp.zeros((1,), stats.dtype), stats[:-1, 3]], 0)
    gradients = jnp.stack([prior_scale * weight * trace_space - 2.0 * prior_scale * correlation * trace_cross, prior_scale * weight_rate * trace_space - 2.0 * prior_scale * complement * trace_cross, noise_scale * trace_data + 2.0 * trace_side]) / NODES
    return (day_sigma, gradients, fixed_sigma)
```

```python
import functools

import jax
import jax.numpy as jnp
from jax import lax
from jax.experimental import pallas as pl
from jax.experimental.pallas import tpu as pltpu
from jax.sharding import PartitionSpec as P

HIGHEST = lax.Precision.HIGHEST
F32 = jnp.float32
BF16 = jnp.bfloat16
VMEM = pl.BlockSpec(memory_space=pltpu.VMEM)
SMEM = pl.BlockSpec(memory_space=pltpu.SMEM)
CLOSE = 1e-6
STEPS = 40


def nn(a, b):
    return lax.dot_general(
        a, b, (((1,), (0,)), ((), ())), precision=HIGHEST, preferred_element_type=F32
    )


def nt(a, b):
    return lax.dot_general(
        a, b, (((1,), (1,)), ((), ())), precision=HIGHEST, preferred_element_type=F32
    )


def coarse(a, b):
    return jnp.dot(a.astype(BF16), b.astype(BF16), preferred_element_type=F32)


def eye(n):
    return (
        lax.broadcasted_iota(jnp.int32, (n, n), 0) == lax.broadcasted_iota(jnp.int32, (n, n), 1)
    ).astype(F32)


def squares(r):
    return jnp.sum(r * r)


def safe_start(a):
    unit = eye(a.shape[0])
    diag_row = jnp.sum(a * unit, axis=0, keepdims=True)
    diag_col = jnp.sum(a * unit, axis=1, keepdims=True)
    scaled = jnp.abs(a) * lax.rsqrt(diag_row) * lax.rsqrt(diag_col)
    bound = jnp.max(jnp.sum(scaled, axis=0, keepdims=True))
    return unit / (diag_row * bound)


def series(x_ref, r_ref):
    def more(state):
        count, size = state
        return (count < 12) & (size > 1e-4)

    def step(state):
        count, _ = state
        r = r_ref[...].astype(BF16)
        x_ref[...] += jnp.dot(r, x_ref[...].astype(BF16), preferred_element_type=F32)
        r_new = jnp.dot(r, r, preferred_element_type=F32)
        r_ref[...] = r_new
        return count + 1, squares(r_new)

    lax.while_loop(more, step, (0, squares(r_ref[...])))


def polish(a, x_ref):
    unit = eye(a.shape[0])

    def more(state):
        count, size, before = state
        return (count < STEPS) & (size > CLOSE) & ((size < before) | (size > 0.5))

    def step(state):
        count, size, _ = state
        r = unit - nn(a, x_ref[...])
        new = squares(r)
        restart = (count == 0) & ~(new < 0.8)

        @pl.when(restart)
        def _():
            x_ref[...] = safe_start(a)

        @pl.when(jnp.logical_not(restart))
        def _():
            x_ref[...] += nn(x_ref[...], r)

        return count + 1, jnp.where(restart, 1e30, new), jnp.where(restart, 2e30, size)

    lax.while_loop(more, step, (0, jnp.float32(1e30), jnp.float32(2e30)))


def first_kernel(s_ref, k_ref, h_ref, z_ref, a_ref, side_ref, x_ref, r_ref):
    h = h_ref[...]
    a = s_ref[0] * k_ref[...] + s_ref[1] * h
    a_ref[...] = a
    side_ref[...] = s_ref[1] * nn(z_ref[...], h)
    start = safe_start(a)
    x_ref[...] = start
    r_ref[...] = eye(a.shape[0]) - jnp.sum(start, axis=1, keepdims=True) * a
    series(x_ref, r_ref)
    polish(a, x_ref)


def update_kernel(last, *refs):
    if last:
        a, l, u, s, xs, ss, xr, sr, a_new, s_new, delta = refs
    else:
        a, l, u, s, xs, ss, xr, sr, ls, ur, a_new, s_new, delta, l_new, u_new = refs
    lv = l[...]
    uv = u[...]
    p = nn(lv, xs[...])
    q = nn(uv, xr[...])
    d = nt(p, lv) + nt(q, uv)
    delta[...] = d
    a_new[...] = a[...] - d
    s_new[...] = s[...] - nt(ss[...], p) - nt(sr[...], q)
    if not last:
        l_new[...] = -nn(p, ls[...])
        u_new[...] = -nn(q, ur[...])


def invert_kernel(a_ref, old_ref, delta_ref, x_ref, r_ref):
    old = old_ref[...]
    x_ref[...] = old
    r_ref[...] = coarse(old, delta_ref[...])
    series(x_ref, r_ref)
    polish(a_ref[...], x_ref)


def packet_kernel(x_ref, s_ref, s0_ref, z_ref, k_ref, h_ref, y_ref, packet_ref):
    x = x_ref[...]
    y = nn(s_ref[...], x)
    y_ref[...] = y
    s0 = s0_ref[...]
    k = k_ref[...]
    h = h_ref[...]
    f = y.shape[0]
    ys = nt(y, s0)
    parts = [nt(s0, z_ref[...]) - ys, nt(nn(y, k), y), nt(nn(y, h), y), ys]
    packet_ref[pl.ds(0, f), :] = jnp.concatenate(parts, axis=1)
    row = lax.broadcasted_iota(jnp.int32, (8, 4 * f), 0)
    packet_ref[pl.ds(f, 8), :] = jnp.where(
        row == 0, jnp.sum(x * k), jnp.where(row == 1, jnp.sum(x * h), 0.0)
    )


def gauss_jordan(m):
    n = m.shape[0]
    rows = lax.broadcasted_iota(jnp.int32, (n, n), 0)
    cols = lax.broadcasted_iota(jnp.int32, (n, n), 1)
    for k in range(n):
        row = m[k : k + 1, :]
        col = m[:, k : k + 1]
        inv = 1.0 / m[k : k + 1, k : k + 1]
        row_s = row * inv
        m_next = m - col * row_s
        m_next = jnp.where(rows == k, row_s, m_next)
        m_next = jnp.where(cols == k, -col * inv, m_next)
        m = jnp.where((rows == k) & (cols == k), inv, m_next)
    return m


def finish_kernel(c_ref, all_ref, prior_ref, x_ref, y_ref, out_ref, grad_ref, fixed_ref):
    n, _, f4 = all_ref.shape
    f = f4 // 4
    extent = x_ref.shape[0]
    packets = all_ref[:, pl.ds(0, f), :]
    total = jnp.sum(packets, axis=0)[:, :f]
    m = eye(f) * prior_ref[...] + total
    sigma = gauss_jordan(m)
    fixed_ref[...] = sigma
    y = y_ref[...]
    sy = nn(sigma, y)
    out_ref[...] = x_ref[...] + lax.dot_general(
        y, sy, (((0,), (0,)), ((), ())), precision=HIGHEST, preferred_element_type=F32
    )
    tiled = jnp.concatenate([sigma] * 4, axis=1)
    v = jnp.sum(packets * tiled[None], axis=1)
    lane = lax.broadcasted_iota(jnp.int32, (n, f4), 1)

    def part(i):
        return jnp.sum(
            jnp.where((lane >= i * f) & (lane < (i + 1) * f), v, 0.0), axis=1, keepdims=True
        )

    tail = all_ref[:, pl.ds(f, 8), :]
    s_col = part(1) + tail[:, 0, 0:1]
    h_col = part(2) + tail[:, 1, 0:1]
    u_col = -part(3)
    tau, rho, noise = c_ref[0], c_ref[1], c_ref[2]
    comp = 1.0 - rho * rho
    t_col = lax.broadcasted_iota(jnp.int32, (n, 1), 0)
    a_col = jnp.where((t_col == 0) | (t_col == n - 1), 1.0, 1.0 + rho * rho)
    g_col = tau * a_col * s_col + noise * h_col + u_col - float(extent)
    j = lax.broadcasted_iota(jnp.int32, (n, n), 0)
    t = lax.broadcasted_iota(jnp.int32, (n, n), 1)
    sign = jnp.where((j + t) % 2 == 1, 1.0, -1.0)
    ahead = jnp.where(j < t, sign, 0.0)
    behind = jnp.where(j >= t, -sign, 0.0)
    weights = jnp.where(t <= n // 2, ahead, behind)
    c_row = jnp.sum(weights * g_col, axis=0, keepdims=True) / (tau * rho)
    unit = eye(n)
    s_row = jnp.sum(unit * s_col, axis=0, keepdims=True)
    h_row = jnp.sum(unit * h_col, axis=0, keepdims=True)
    u_row = jnp.sum(unit * u_col, axis=0, keepdims=True)
    t_row = lax.broadcasted_iota(jnp.int32, (1, n), 1)
    border = (t_row == 0) | (t_row == n - 1)
    a_row = jnp.where(border, 1.0, 1.0 + rho * rho)
    b_row = jnp.where(border, 0.0, 2.0 * rho * comp)
    scale = 1.0 / extent
    grad_ref[pl.ds(0, 1), :] = (tau * a_row * s_row - 2.0 * tau * rho * c_row) * scale
    grad_ref[pl.ds(1, 1), :] = (tau * b_row * s_row - 2.0 * tau * comp * c_row) * scale
    grad_ref[pl.ds(2, 1), :] = (noise * h_row + 2.0 * u_row) * scale


def shaped(*shapes):
    return [jax.ShapeDtypeStruct(s, F32) for s in shapes]


def on_device(hyper_params, space_precision, data_precision, covariates, fixed_precision):
    core = lax.axis_index("blk")
    position = lax.axis_index("tm")
    n = 2 * lax.axis_size("tm")
    half, extent = space_precision.shape
    fixed = covariates.shape[1]
    day = 2 * position + core
    axes = ("tm", "blk")
    swap = [(0, 1), (1, 0)]

    def mine(x, c):
        return lax.dynamic_index_in_dim(x, c, 0, keepdims=False)

    def joined(own, other, axis):
        low = jnp.where(core == 0, own, other)
        high = jnp.where(core == 0, other, own)
        return jnp.concatenate([low, high], axis)

    sent = jnp.concatenate([mine(data_precision, 1 - core), space_precision], 0)
    got = lax.ppermute(sent, "blk", swap)
    got_z = lax.ppermute(mine(covariates, 1 - core), "blk", swap)
    k = joined(space_precision, got[half:], 0)
    h = joined(mine(data_precision, core), got[:half], 0)
    z = joined(mine(covariates, core), got_z, 1)

    tau = jnp.exp(hyper_params[0])
    rho = jnp.tanh(hyper_params[1])
    noise = jnp.exp(hyper_params[2])
    weight = jnp.where((day == 0) | (day == n - 1), 1.0, 1.0 + rho * rho)
    scalars = jnp.stack([tau * weight, noise])
    couple = -tau * rho * k

    def gate(flag):
        return jnp.where(flag, couple, 0.0)

    square = (extent, extent)
    side = (fixed, extent)
    a, s0, x = pl.pallas_call(
        first_kernel,
        out_shape=shaped(square, side, square),
        in_specs=[SMEM, VMEM, VMEM, VMEM],
        out_specs=[VMEM] * 3,
        scratch_shapes=[pltpu.VMEM(square, F32)],
    )(scalars, k, h, z)
    s = s0
    l, u = gate(day >= 1), gate(day <= n - 2)
    ls, ur = gate(day >= 2), gate(day <= n - 3)

    distance = 1
    while distance < n:
        last = 2 * distance >= n
        up = [(i, i + distance) for i in range(n - distance)]
        down = [(i + distance, i) for i in range(n - distance)]
        if distance > 1 and not last:
            ls, ur = lax.ppermute(l, axes, up), lax.ppermute(u, axes, down)
        ss, sr = lax.ppermute(s, axes, up), lax.ppermute(s, axes, down)
        xs, xr = lax.ppermute(x, axes, up), lax.ppermute(x, axes, down)
        args = [a, l, u, s, xs, ss, xr, sr] + ([] if last else [ls, ur])
        outs = shaped(square, side, square) + ([] if last else shaped(square, square))
        res = pl.pallas_call(
            functools.partial(update_kernel, last),
            out_shape=outs,
            in_specs=[VMEM] * len(args),
            out_specs=[VMEM] * len(outs),
        )(*args)
        a, s, delta = res[:3]
        if not last:
            l, u = res[3:]
        x = pl.pallas_call(
            invert_kernel,
            out_shape=shaped(square)[0],
            in_specs=[VMEM] * 3,
            out_specs=VMEM,
            scratch_shapes=[pltpu.VMEM(square, F32)],
        )(a, x, delta)
        distance *= 2

    y, packet = pl.pallas_call(
        packet_kernel,
        out_shape=shaped(side, (fixed + 8, 4 * fixed)),
        in_specs=[VMEM] * 6,
        out_specs=[VMEM] * 2,
    )(x, s, s0, z, k, h)
    everyone = lax.all_gather(packet, axes, axis=0)
    out, grads, sigma = pl.pallas_call(
        finish_kernel,
        out_shape=shaped(square, (3, n), (fixed, fixed)),
        in_specs=[SMEM] + [VMEM] * 4,
        out_specs=[VMEM] * 3,
    )(jnp.stack([tau, rho, noise]), everyone, fixed_precision[None], x, y)
    gradients = lax.dynamic_slice_in_dim(grads, 2 * position, 2, 1)
    own_rows = lax.dynamic_slice_in_dim(out, core * half, half, 0)
    other_rows = lax.dynamic_slice_in_dim(out, (1 - core) * half, half, 0)
    got_rows = lax.ppermute(other_rows, "blk", swap)
    low = jnp.where(core == 0, own_rows, got_rows)
    high = jnp.where(core == 0, got_rows, own_rows)
    return jnp.stack([low, high]), gradients, sigma


def solution(mesh):
    in_specs = (
        P("grp"),
        P("blk", None),
        P(("grp", "tm"), "blk", None),
        P(("grp", "tm"), None, "blk"),
        P("grp"),
    )
    out_specs = (P(("grp", "tm"), "blk", None), P(None, ("grp", "tm")), P("grp", None))
    return jax.shard_map(
        on_device, mesh=mesh, in_specs=in_specs, out_specs=out_specs, check_vma=False
    )
```

```python
import functools

import jax
import jax.numpy as jnp
from jax import lax
from jax.experimental import pallas as pl
from jax.experimental.pallas import tpu as pltpu
from jax.sharding import PartitionSpec as P

HIGHEST = lax.Precision.HIGHEST
F32 = jnp.float32
BF16 = jnp.bfloat16
VMEM = pl.BlockSpec(memory_space=pltpu.VMEM)
SMEM = pl.BlockSpec(memory_space=pltpu.SMEM)
CLOSE = 1e-6
STEPS = 40
DOUBLINGS = 5
MESH = pl.DeviceIdType.MESH


def nn(a, b):
    return lax.dot_general(
        a, b, (((1,), (0,)), ((), ())), precision=HIGHEST, preferred_element_type=F32
    )


def nt(a, b):
    return lax.dot_general(
        a, b, (((1,), (1,)), ((), ())), precision=HIGHEST, preferred_element_type=F32
    )


def eye(n):
    return (
        lax.broadcasted_iota(jnp.int32, (n, n), 0) == lax.broadcasted_iota(jnp.int32, (n, n), 1)
    ).astype(F32)


def squares(r):
    return jnp.sum(r * r)


def safe_start(a):
    unit = eye(a.shape[0])
    diag_row = jnp.sum(a * unit, axis=0, keepdims=True)
    diag_col = jnp.sum(a * unit, axis=1, keepdims=True)
    scaled = jnp.abs(a) * lax.rsqrt(diag_row) * lax.rsqrt(diag_col)
    bound = jnp.max(jnp.sum(scaled, axis=0, keepdims=True))
    return unit / (diag_row * bound)


def series(x_ref, r_ref):
    def more(state):
        count, size = state
        return (count < 12) & (size > 1e-4)

    def step(state):
        count, _ = state
        r = r_ref[...].astype(BF16)
        x_ref[...] += jnp.dot(r, x_ref[...].astype(BF16), preferred_element_type=F32)
        r_new = jnp.dot(r, r, preferred_element_type=F32)
        r_ref[...] = r_new
        return count + 1, squares(r_new)

    lax.while_loop(more, step, (0, squares(r_ref[...])))


def polish(a, x_ref):
    unit = eye(a.shape[0])

    def more(state):
        count, size, before = state
        return (count < STEPS) & (size > CLOSE) & ((size < before) | (size > 0.5))

    def step(state):
        count, size, _ = state
        r = unit - nn(a, x_ref[...])
        new = squares(r)
        restart = (count == 0) & ~(new < 0.8)

        @pl.when(restart)
        def _():
            x_ref[...] = safe_start(a)

        @pl.when(jnp.logical_not(restart))
        def _():
            x_ref[...] += nn(x_ref[...], r)

        return count + 1, jnp.where(restart, 1e30, new), jnp.where(restart, 2e30, size)

    lax.while_loop(more, step, (0, jnp.float32(1e30), jnp.float32(2e30)))


def split(a):
    high = a.astype(BF16)
    return high, (a - high.astype(F32)).astype(BF16)


def bdot(a, b):
    return jnp.dot(a, b, preferred_element_type=F32)


def three(a, b):
    ah, al = split(a)
    bh, bl = split(b)
    return bdot(ah, bh) + (bdot(ah, bl) + bdot(al, bh))


def first_kernel(a_ref, x_ref, r_ref):
    a = a_ref[...]
    start = safe_start(a)
    x_ref[...] = start
    r_ref[...] = eye(a.shape[0]) - jnp.sum(start, axis=1, keepdims=True) * a
    series(x_ref, r_ref)
    polish(a, x_ref)


def exchange_kernel(c_ref, space, data, cov, k_ref, h_ref, z_ref, a_ref, s_ref, ssem, rsem):
    core = lax.axis_index("blk")
    peer = {"blk": 1 - core}
    half = space.shape[0]
    barrier = pltpu.get_barrier_semaphore()
    pl.semaphore_signal(barrier, inc=1, device_id=peer, device_id_type=MESH)
    pl.semaphore_wait(barrier, 1)
    own = pl.ds(pl.multiple_of(core * half, half), half)
    sends = [
        (space, k_ref.at[own, :]),
        (data.at[1 - core], h_ref.at[own, :]),
        (cov.at[1 - core], z_ref.at[:, own]),
    ]
    copies = [
        pltpu.make_async_remote_copy(
            src_ref=src,
            dst_ref=dst,
            send_sem=ssem.at[i],
            recv_sem=rsem.at[i],
            device_id=peer,
            device_id_type=MESH,
        )
        for i, (src, dst) in enumerate(sends)
    ]
    for copy in copies:
        copy.start()
    k_ref[own, :] = space[...]
    h_ref[own, :] = data[core]
    z_ref[:, own] = cov[core]
    for copy in copies:
        copy.wait()
    h = h_ref[...]
    a_ref[...] = c_ref[3] * k_ref[...] + c_ref[2] * h
    s_ref[...] = c_ref[2] * nn(z_ref[...], h)


def warm_inverse(a, old, delta):
    x = old
    r = three(old, delta)
    for step in range(DOUBLINGS):
        rh, rl = split(r)
        xh, xl = split(x)
        x = x + (bdot(rh, xh) + (bdot(rh, xl) + bdot(rl, xh)))
        if step < DOUBLINGS - 1:
            r = bdot(rh, rh) + (bdot(rh, rl) + bdot(rl, rh))
    residual = eye(a.shape[0]) - nn(a, x)
    return x + three(x, residual)


def main_kernel(levels, c_ref, k_ref, h_ref, z_ref, a_in, s0_ref, x0_ref, prior_ref, *rest):
    out_ref, grad_ref, fixed_ref = rest[:3]
    xo, lo, uo, so, xs, xr, ls, ur, ss, sr, all_ref, full, ssem, rsem, psend, precv, hsem = rest[3:]
    n = 1 << levels
    core = lax.axis_index("blk")
    position = lax.axis_index("tm")
    day = 2 * position + core
    half = out_ref.shape[1]
    f = s0_ref.shape[0]

    def device(t):
        return {"tm": t // 2, "blk": t % 2}

    barrier = pltpu.get_barrier_semaphore()

    @pl.loop(1, n)
    def _(o):
        pl.semaphore_signal(
            barrier, inc=1, device_id=device((day + o) % n), device_id_type=MESH
        )

    pl.semaphore_wait(barrier, n - 1)

    def transfer(src, dst, level, slot, t):
        return pltpu.make_async_remote_copy(
            src_ref=src,
            dst_ref=dst,
            send_sem=ssem.at[level, slot],
            recv_sem=rsem.at[level, slot],
            device_id=device(t),
            device_id_type=MESH,
        )

    def route(level, which):
        d = 1 << level
        if which == 0:
            src = x0_ref if level == 0 else xo.at[level - 1]
            pair = ((src, xs.at[level]), (src, xr.at[level]))
        elif which == 1:
            src = s0_ref if level == 0 else so.at[level - 1]
            pair = ((src, ss.at[level]), (src, sr.at[level]))
        else:
            pair = ((lo.at[level], ls.at[level]), (uo.at[level], ur.at[level]))
        later = transfer(*pair[0], level, 2 * which, (day + d) % n)
        earlier = transfer(*pair[1], level, 2 * which + 1, (day + n - d) % n)
        return d, later, earlier, pair[0][1], pair[1][1]

    def send(level, which):
        d, later, earlier, low, high = route(level, which)

        @pl.when(day + d < n)
        def _():
            later.start()

        @pl.when(day >= d)
        def _():
            earlier.start()

    def receive(level, which):
        d, later, earlier, low, high = route(level, which)

        @pl.when(day >= d)
        def _():
            later.wait_recv()

        @pl.when(day < d)
        def _():
            low[...] = jnp.zeros_like(low)

        @pl.when(day + d < n)
        def _():
            earlier.wait_recv()

        @pl.when(day + d >= n)
        def _():
            high[...] = jnp.zeros_like(high)

    def sent(level, which):
        d, later, earlier, low, high = route(level, which)

        @pl.when(day + d < n)
        def _():
            later.wait_send()

        @pl.when(day >= d)
        def _():
            earlier.wait_send()

    send(0, 0)
    send(0, 1)
    k = k_ref[...]
    couple = -(c_ref[0] * c_ref[1]) * k

    def gate(flag):
        return jnp.where(flag, 1.0, 0.0) * couple

    lo[0] = gate(day >= 1)
    uo[0] = gate(day <= n - 2)
    ls[0] = gate(day >= 2)
    ur[0] = gate(day <= n - 3)
    a = a_in[...]
    s = s0_ref[...]
    x = x0_ref[...]
    for level in range(levels):
        last = level == levels - 1
        receive(level, 0)
        l = lo[level]
        u = uo[level]
        p = nn(l, xs[level])
        q = nn(u, xr[level])
        delta = nt(p, l) + nt(q, u)
        receive(level, 1)
        s = s - nt(ss[level], p) - nt(sr[level], q)
        a = a - delta
        if not last:
            so[level] = s
            send(level + 1, 1)
            if level > 0:
                receive(level, 2)
            lo[level + 1] = -nn(p, ls[level])
            uo[level + 1] = -nn(q, ur[level])
            if level + 1 < levels - 1:
                send(level + 1, 2)
        x = warm_inverse(a, x, delta)
        if not last:
            xo[level] = x
            send(level + 1, 0)

    y = nn(s, x)
    s0 = s0_ref[...]
    h = h_ref[...]
    ys = nt(y, s0)
    parts = [nt(s0, z_ref[...]) - ys, nt(nn(y, k), y), nt(nn(y, h), y), ys]
    all_ref[day, pl.ds(0, f), :] = jnp.concatenate(parts, axis=1)
    line = lax.broadcasted_iota(jnp.int32, (8, 4 * f), 0)
    all_ref[day, pl.ds(f, 8), :] = jnp.where(
        line == 0, jnp.sum(x * k), jnp.where(line == 1, jnp.sum(x * h), 0.0)
    )

    def packet(to, slot):
        return pltpu.make_async_remote_copy(
            src_ref=all_ref.at[day],
            dst_ref=all_ref.at[slot],
            send_sem=psend.at[to],
            recv_sem=precv.at[slot],
            device_id=device(to),
            device_id_type=MESH,
        )

    @pl.loop(1, n)
    def _(o):
        packet((day + o) % n, day).start()

    @pl.loop(1, n)
    def _(o):
        packet((day + o) % n, (day + o) % n).wait_recv()

    finish(c_ref, all_ref, prior_ref, x, y, full, grad_ref, fixed_ref)
    swap = pltpu.make_async_remote_copy(
        src_ref=full.at[pl.ds(pl.multiple_of((1 - core) * half, half), half), :],
        dst_ref=out_ref.at[core],
        send_sem=hsem.at[0],
        recv_sem=hsem.at[1],
        device_id={"blk": 1 - core},
        device_id_type=MESH,
    )
    swap.start()
    out_ref[core] = full[pl.ds(pl.multiple_of(core * half, half), half), :]

    @pl.loop(1, n)
    def _(o):
        packet((day + o) % n, day).wait_send()

    for level in range(levels):
        sent(level, 0)
        sent(level, 1)
        if 0 < level < levels - 1:
            sent(level, 2)
    swap.wait()


def gauss_jordan(m):
    n = m.shape[0]
    rows = lax.broadcasted_iota(jnp.int32, (n, n), 0)
    cols = lax.broadcasted_iota(jnp.int32, (n, n), 1)
    for k in range(n):
        row = m[k : k + 1, :]
        col = m[:, k : k + 1]
        inv = 1.0 / m[k : k + 1, k : k + 1]
        row_s = row * inv
        m_next = m - col * row_s
        m_next = jnp.where(rows == k, row_s, m_next)
        m_next = jnp.where(cols == k, -col * inv, m_next)
        m = jnp.where((rows == k) & (cols == k), inv, m_next)
    return m


def finish(c_ref, all_ref, prior_ref, x, y, out_ref, grad_ref, fixed_ref):
    n, _, f4 = all_ref.shape
    f = f4 // 4
    extent = x.shape[0]
    packets = all_ref[:, pl.ds(0, f), :]
    total = jnp.sum(packets, axis=0)[:, :f]
    m = eye(f) * prior_ref[...] + total
    sigma = gauss_jordan(m)
    fixed_ref[...] = sigma
    sy = nn(sigma, y)
    out_ref[...] = x + lax.dot_general(
        y, sy, (((0,), (0,)), ((), ())), precision=HIGHEST, preferred_element_type=F32
    )
    tiled = jnp.concatenate([sigma] * 4, axis=1)
    v = jnp.sum(packets * tiled[None], axis=1)
    lane = lax.broadcasted_iota(jnp.int32, (n, f4), 1)

    def part(i):
        return jnp.sum(
            jnp.where((lane >= i * f) & (lane < (i + 1) * f), v, 0.0), axis=1, keepdims=True
        )

    tail = all_ref[:, pl.ds(f, 8), :]
    s_col = part(1) + tail[:, 0, 0:1]
    h_col = part(2) + tail[:, 1, 0:1]
    u_col = -part(3)
    tau, rho, noise = c_ref[0], c_ref[1], c_ref[2]
    comp = 1.0 - rho * rho
    t_col = lax.broadcasted_iota(jnp.int32, (n, 1), 0)
    a_col = jnp.where((t_col == 0) | (t_col == n - 1), 1.0, 1.0 + rho * rho)
    g_col = tau * a_col * s_col + noise * h_col + u_col - float(extent)
    j = lax.broadcasted_iota(jnp.int32, (n, n), 0)
    t = lax.broadcasted_iota(jnp.int32, (n, n), 1)
    sign = jnp.where((j + t) % 2 == 1, 1.0, -1.0)
    ahead = jnp.where(j < t, sign, 0.0)
    behind = jnp.where(j >= t, -sign, 0.0)
    weights = jnp.where(t <= n // 2, ahead, behind)
    c_row = jnp.sum(weights * g_col, axis=0, keepdims=True) / (tau * rho)
    unit = eye(n)
    s_row = jnp.sum(unit * s_col, axis=0, keepdims=True)
    h_row = jnp.sum(unit * h_col, axis=0, keepdims=True)
    u_row = jnp.sum(unit * u_col, axis=0, keepdims=True)
    t_row = lax.broadcasted_iota(jnp.int32, (1, n), 1)
    border = (t_row == 0) | (t_row == n - 1)
    a_row = jnp.where(border, 1.0, 1.0 + rho * rho)
    b_row = jnp.where(border, 0.0, 2.0 * rho * comp)
    scale = 1.0 / extent
    rows = [
        (tau * a_row * s_row - 2.0 * tau * rho * c_row) * scale,
        (tau * b_row * s_row - 2.0 * tau * comp * c_row) * scale,
        (noise * h_row + 2.0 * u_row) * scale,
    ]
    first = 2 * lax.axis_index("tm")
    two = lax.broadcasted_iota(jnp.int32, (1, 2), 1)
    for i, row in enumerate(rows):
        low = jnp.sum(jnp.where(t_row == first, row, 0.0), axis=1, keepdims=True)
        high = jnp.sum(jnp.where(t_row == first + 1, row, 0.0), axis=1, keepdims=True)
        grad_ref[pl.ds(i, 1), :] = jnp.where(two == 0, low, high)


def shaped(*shapes):
    return [jax.ShapeDtypeStruct(s, F32) for s in shapes]


def on_device(hyper_params, space_precision, data_precision, covariates, fixed_precision):
    n = 2 * lax.axis_size("tm")
    levels = n.bit_length() - 1
    half, extent = space_precision.shape
    fixed = covariates.shape[1]
    day = 2 * lax.axis_index("tm") + lax.axis_index("blk")
    tau = jnp.exp(hyper_params[0])
    rho = jnp.tanh(hyper_params[1])
    noise = jnp.exp(hyper_params[2])
    weight = jnp.where((day == 0) | (day == n - 1), 1.0, 1.0 + rho * rho)
    scalars = jnp.stack([tau, rho, noise, tau * weight])
    square = (extent, extent)
    side = (fixed, extent)
    k, h, z, a, s0 = pl.pallas_call(
        exchange_kernel,
        out_shape=shaped(square, square, side, square, side),
        in_specs=[SMEM] + [VMEM] * 3,
        out_specs=[VMEM] * 5,
        scratch_shapes=[pltpu.SemaphoreType.DMA((3,)), pltpu.SemaphoreType.DMA((3,))],
        compiler_params=pltpu.CompilerParams(collective_id=0, has_side_effects=True),
    )(scalars, space_precision, data_precision, covariates)
    x = pl.pallas_call(
        first_kernel,
        out_shape=shaped(square)[0],
        in_specs=[VMEM],
        out_specs=VMEM,
        scratch_shapes=[pltpu.VMEM(square, F32)],
    )(a)
    return pl.pallas_call(
        functools.partial(main_kernel, levels),
        out_shape=shaped((2, half, extent), (3, 2), (fixed, fixed)),
        in_specs=[SMEM] + [VMEM] * 7,
        out_specs=[VMEM] * 3,
        scratch_shapes=[pltpu.VMEM((levels,) + square, F32)] * 3
        + [pltpu.VMEM((levels,) + side, F32)]
        + [pltpu.VMEM((levels,) + square, F32)] * 4
        + [pltpu.VMEM((levels,) + side, F32)] * 2
        + [
            pltpu.VMEM((n, fixed + 8, 4 * fixed), F32),
            pltpu.VMEM(square, F32),
            pltpu.SemaphoreType.DMA((levels, 6)),
            pltpu.SemaphoreType.DMA((levels, 6)),
            pltpu.SemaphoreType.DMA((n,)),
            pltpu.SemaphoreType.DMA((n,)),
            pltpu.SemaphoreType.DMA((2,)),
        ],
        compiler_params=pltpu.CompilerParams(
            collective_id=1, has_side_effects=True, vmem_limit_bytes=48 * 1024 * 1024
        ),
    )(scalars, k, h, z, a, s0, x, fixed_precision[None])


def solution(mesh):
    in_specs = (
        P("grp"),
        P("blk", None),
        P(("grp", "tm"), "blk", None),
        P(("grp", "tm"), None, "blk"),
        P("grp"),
    )
    out_specs = (P(("grp", "tm"), "blk", None), P(None, ("grp", "tm")), P("grp", None))
    return jax.shard_map(
        on_device, mesh=mesh, in_specs=in_specs, out_specs=out_specs, check_vma=False
    )
```

```python
import functools

import jax
import jax.numpy as jnp
from jax import lax
from jax.experimental import pallas as pl
from jax.experimental.pallas import tpu as pltpu
from jax.sharding import PartitionSpec as P

HIGHEST = lax.Precision.HIGHEST
F32 = jnp.float32
BF16 = jnp.bfloat16
VMEM = pl.BlockSpec(memory_space=pltpu.VMEM)
SMEM = pl.BlockSpec(memory_space=pltpu.SMEM)
CLOSE = 1e-6
STEPS = 40
DOUBLINGS = 5
MESH = pl.DeviceIdType.MESH


def nn(a, b):
    return three(a, b)


def nt(a, b):
    ah, al = split(a)
    bh, bl = split(b)
    return bdot_t(ah, bh) + (bdot_t(ah, bl) + bdot_t(al, bh))


def full_dot(a, b):
    return jnp.dot(a, b, precision=HIGHEST, preferred_element_type=F32)


def eye(n):
    return (
        lax.broadcasted_iota(jnp.int32, (n, n), 0) == lax.broadcasted_iota(jnp.int32, (n, n), 1)
    ).astype(F32)


def squares(r):
    return jnp.sum(r * r)


def safe_start(a):
    unit = eye(a.shape[0])
    diag_row = jnp.sum(a * unit, axis=0, keepdims=True)
    diag_col = jnp.sum(a * unit, axis=1, keepdims=True)
    scaled = jnp.abs(a) * lax.rsqrt(diag_row) * lax.rsqrt(diag_col)
    bound = jnp.max(jnp.sum(scaled, axis=0, keepdims=True))
    return unit / (diag_row * bound)


def series(x_ref, r_ref):
    def more(state):
        count, size = state
        return (count < 12) & (size > 1e-4)

    def step(state):
        count, _ = state
        r = r_ref[...].astype(BF16)
        x_ref[...] += jnp.dot(r, x_ref[...].astype(BF16), preferred_element_type=F32)
        r_new = jnp.dot(r, r, preferred_element_type=F32)
        r_ref[...] = r_new
        return count + 1, squares(r_new)

    lax.while_loop(more, step, (0, squares(r_ref[...])))


def polish(a, x_ref):
    unit = eye(a.shape[0])

    def more(state):
        count, size, before = state
        return (count < STEPS) & (size > CLOSE) & ((size < before) | (size > 0.5))

    def step(state):
        count, size, _ = state
        r = unit - full_dot(a, x_ref[...])
        new = squares(r)
        restart = (count == 0) & ~(new < 0.8)

        @pl.when(restart)
        def _():
            x_ref[...] = safe_start(a)

        @pl.when(jnp.logical_not(restart))
        def _():
            x_ref[...] += nn(x_ref[...], r)

        return count + 1, jnp.where(restart, 1e30, new), jnp.where(restart, 2e30, size)

    lax.while_loop(more, step, (0, jnp.float32(1e30), jnp.float32(2e30)))


def split(a):
    high = a.astype(BF16)
    return high, (a - high.astype(F32)).astype(BF16)


def bdot_t(a, b):
    return lax.dot_general(a, b, (((1,), (1,)), ((), ())), preferred_element_type=F32)


def bdot(a, b):
    return jnp.dot(a, b, preferred_element_type=F32)


def three(a, b):
    ah, al = split(a)
    bh, bl = split(b)
    return bdot(ah, bh) + (bdot(ah, bl) + bdot(al, bh))


def first_kernel(a_ref, x_ref, r_ref):
    a = a_ref[...]
    start = safe_start(a)
    x_ref[...] = start
    r_ref[...] = eye(a.shape[0]) - jnp.sum(start, axis=1, keepdims=True) * a
    series(x_ref, r_ref)
    polish(a, x_ref)


def exchange_kernel(c_ref, space, data, cov, k_ref, h_ref, z_ref, a_ref, s_ref, ssem, rsem):
    core = lax.axis_index("blk")
    peer = {"blk": 1 - core}
    half = space.shape[0]
    barrier = pltpu.get_barrier_semaphore()
    pl.semaphore_signal(barrier, inc=1, device_id=peer, device_id_type=MESH)
    pl.semaphore_wait(barrier, 1)
    own = pl.ds(pl.multiple_of(core * half, half), half)
    sends = [
        (space, k_ref.at[own, :]),
        (data.at[1 - core], h_ref.at[own, :]),
        (cov.at[1 - core], z_ref.at[:, own]),
    ]
    copies = [
        pltpu.make_async_remote_copy(
            src_ref=src,
            dst_ref=dst,
            send_sem=ssem.at[i],
            recv_sem=rsem.at[i],
            device_id=peer,
            device_id_type=MESH,
        )
        for i, (src, dst) in enumerate(sends)
    ]
    for copy in copies:
        copy.start()
    k_ref[own, :] = space[...]
    h_ref[own, :] = data[core]
    z_ref[:, own] = cov[core]
    for copy in copies:
        copy.wait()
    h = h_ref[...]
    a_ref[...] = c_ref[3] * k_ref[...] + c_ref[2] * h
    s_ref[...] = c_ref[2] * nn(z_ref[...], h)


def warm_inverse(a, old, delta):
    x = old
    r = three(old, delta)
    for step in range(DOUBLINGS):
        rh, rl = split(r)
        xh, xl = split(x)
        x = x + (bdot(rh, xh) + (bdot(rh, xl) + bdot(rl, xh)))
        if step < DOUBLINGS - 1:
            r = bdot(rh, rh) + (bdot(rh, rl) + bdot(rl, rh))
    residual = eye(a.shape[0]) - nn(a, x)
    return x + three(x, residual)


def pack(ref, x):
    n = x.shape[0]
    half = n // 2
    ref[pl.ds(0, n), :] = x[:, :half]
    ref[pl.ds(n, half), :] = x[half:, half:]


def unpack(ref):
    half = ref.shape[-1]
    left = ref[pl.ds(0, 2 * half), :]
    right = jnp.concatenate([left[half:, :].T, ref[pl.ds(2 * half, half), :]], axis=0)
    return jnp.concatenate([left, right], axis=1)


def main_kernel(levels, c_ref, k_ref, h_ref, z_ref, a_in, s0_ref, x0_ref, prior_ref, *rest):
    out_ref, grad_ref, fixed_ref = rest[:3]
    xo, lo, uo, so, xs, xr, ls, ur, ss, sr, early, all_ref, full, *sems = rest[3:]
    ssem, rsem, psend, precv, hsem = sems
    n = 1 << levels
    core = lax.axis_index("blk")
    position = lax.axis_index("tm")
    day = 2 * position + core
    half = out_ref.shape[1]
    f = s0_ref.shape[0]

    def device(t):
        return {"tm": t // 2, "blk": t % 2}

    barrier = pltpu.get_barrier_semaphore()

    @pl.loop(1, n)
    def _(o):
        pl.semaphore_signal(
            barrier, inc=1, device_id=device((day + o) % n), device_id_type=MESH
        )

    pl.semaphore_wait(barrier, n - 1)

    def transfer(src, dst, level, slot, t):
        return pltpu.make_async_remote_copy(
            src_ref=src,
            dst_ref=dst,
            send_sem=ssem.at[level, slot],
            recv_sem=rsem.at[level, slot],
            device_id=device(t),
            device_id_type=MESH,
        )

    def route(level, which):
        d = 1 << level
        if which == 0:
            src = xo.at[level]
            pair = ((src, xs.at[level]), (src, xr.at[level]))
        elif which == 1:
            src = s0_ref if level == 0 else so.at[level - 1]
            pair = ((src, ss.at[level]), (src, sr.at[level]))
        elif level == 1:
            pair = ((early.at[0], early.at[2]), (early.at[1], early.at[3]))
        else:
            pair = ((lo.at[level], ls.at[level]), (uo.at[level], ur.at[level]))
        later = transfer(*pair[0], level, 2 * which, (day + d) % n)
        earlier = transfer(*pair[1], level, 2 * which + 1, (day + n - d) % n)
        return d, later, earlier, pair[0][1], pair[1][1]

    def send(level, which):
        d, later, earlier, low, high = route(level, which)

        @pl.when(day + d < n)
        def _():
            later.start()

        @pl.when(day >= d)
        def _():
            earlier.start()

    def receive(level, which):
        d, later, earlier, low, high = route(level, which)

        @pl.when(day >= d)
        def _():
            later.wait_recv()

        @pl.when(day < d)
        def _():
            low[...] = jnp.zeros_like(low)

        @pl.when(day + d < n)
        def _():
            earlier.wait_recv()

        @pl.when(day + d >= n)
        def _():
            high[...] = jnp.zeros_like(high)

    def sent(level, which):
        d, later, earlier, low, high = route(level, which)

        @pl.when(day + d < n)
        def _():
            later.wait_send()

        @pl.when(day >= d)
        def _():
            earlier.wait_send()

    pack(xo.at[0], x0_ref[...])
    send(0, 0)
    send(0, 1)
    k = k_ref[...]
    couple = -(c_ref[0] * c_ref[1]) * k

    def gate(flag):
        return jnp.where(flag, 1.0, 0.0) * couple

    lo[0] = gate(day >= 1)
    uo[0] = gate(day <= n - 2)
    ls[0] = gate(day >= 2)
    ur[0] = gate(day <= n - 3)
    a = a_in[...]
    s = s0_ref[...]
    x = x0_ref[...]
    for level in range(levels):
        last = level == levels - 1
        receive(level, 0)
        l = lo[level]
        u = uo[level]
        p = nn(l, unpack(xs.at[level]))
        q = nn(u, unpack(xr.at[level]))
        delta = nt(p, l) + nt(q, u)
        receive(level, 1)
        s = s - nt(ss[level], p) - nt(sr[level], q)
        a = a - delta
        if not last:
            so[level] = s
            send(level + 1, 1)
            if level > 0:
                receive(level, 2)
            l_far = unpack(early.at[2]) if level == 1 else ls[level]
            u_far = unpack(early.at[3]) if level == 1 else ur[level]
            l_new = -nn(p, l_far)
            u_new = -nn(q, u_far)
            lo[level + 1] = l_new
            uo[level + 1] = u_new
            if level == 0:
                pack(early.at[0], l_new)
                pack(early.at[1], u_new)
            if level + 1 < levels - 1:
                send(level + 1, 2)
        x = warm_inverse(a, x, delta)
        if not last:
            pack(xo.at[level + 1], x)
            send(level + 1, 0)

    y = nn(s, x)
    s0 = s0_ref[...]
    h = h_ref[...]
    ys = nt(y, s0)
    parts = [nt(s0, z_ref[...]) - ys, nt(nn(y, k), y), nt(nn(y, h), y), ys]
    all_ref[day, pl.ds(0, f), :] = jnp.concatenate(parts, axis=1)
    line = lax.broadcasted_iota(jnp.int32, (8, 4 * f), 0)
    all_ref[day, pl.ds(f, 8), :] = jnp.where(
        line == 0, jnp.sum(x * k), jnp.where(line == 1, jnp.sum(x * h), 0.0)
    )

    def packet(to, slot):
        return pltpu.make_async_remote_copy(
            src_ref=all_ref.at[day],
            dst_ref=all_ref.at[slot],
            send_sem=psend.at[to],
            recv_sem=precv.at[slot],
            device_id=device(to),
            device_id_type=MESH,
        )

    @pl.loop(1, n)
    def _(o):
        packet((day + o) % n, day).start()

    @pl.loop(1, n)
    def _(o):
        packet((day + o) % n, (day + o) % n).wait_recv()

    finish(c_ref, all_ref, prior_ref, x, y, full, grad_ref, fixed_ref)
    swap = pltpu.make_async_remote_copy(
        src_ref=full.at[pl.ds(pl.multiple_of((1 - core) * half, half), half), :],
        dst_ref=out_ref.at[core],
        send_sem=hsem.at[0],
        recv_sem=hsem.at[1],
        device_id={"blk": 1 - core},
        device_id_type=MESH,
    )
    swap.start()
    out_ref[core] = full[pl.ds(pl.multiple_of(core * half, half), half), :]

    @pl.loop(1, n)
    def _(o):
        packet((day + o) % n, day).wait_send()

    for level in range(levels):
        sent(level, 0)
        sent(level, 1)
        if 0 < level < levels - 1:
            sent(level, 2)
    swap.wait()


def gauss_jordan(m):
    n = m.shape[0]
    rows = lax.broadcasted_iota(jnp.int32, (n, n), 0)
    cols = lax.broadcasted_iota(jnp.int32, (n, n), 1)
    for k in range(n):
        row = m[k : k + 1, :]
        col = m[:, k : k + 1]
        inv = 1.0 / m[k : k + 1, k : k + 1]
        row_s = row * inv
        m_next = m - col * row_s
        m_next = jnp.where(rows == k, row_s, m_next)
        m_next = jnp.where(cols == k, -col * inv, m_next)
        m = jnp.where((rows == k) & (cols == k), inv, m_next)
    return m


def finish(c_ref, all_ref, prior_ref, x, y, out_ref, grad_ref, fixed_ref):
    n, _, f4 = all_ref.shape
    f = f4 // 4
    extent = x.shape[0]
    packets = all_ref[:, pl.ds(0, f), :]
    total = jnp.sum(packets, axis=0)[:, :f]
    m = eye(f) * prior_ref[...] + total
    sigma = gauss_jordan(m)
    fixed_ref[...] = sigma
    sy = nn(sigma, y)
    out_ref[...] = x + lax.dot_general(
        y, sy, (((0,), (0,)), ((), ())), precision=HIGHEST, preferred_element_type=F32
    )
    tiled = jnp.concatenate([sigma] * 4, axis=1)
    v = jnp.sum(packets * tiled[None], axis=1)
    lane = lax.broadcasted_iota(jnp.int32, (n, f4), 1)

    def part(i):
        return jnp.sum(
            jnp.where((lane >= i * f) & (lane < (i + 1) * f), v, 0.0), axis=1, keepdims=True
        )

    tail = all_ref[:, pl.ds(f, 8), :]
    s_col = part(1) + tail[:, 0, 0:1]
    h_col = part(2) + tail[:, 1, 0:1]
    u_col = -part(3)
    tau, rho, noise = c_ref[0], c_ref[1], c_ref[2]
    comp = 1.0 - rho * rho
    t_col = lax.broadcasted_iota(jnp.int32, (n, 1), 0)
    a_col = jnp.where((t_col == 0) | (t_col == n - 1), 1.0, 1.0 + rho * rho)
    g_col = tau * a_col * s_col + noise * h_col + u_col - float(extent)
    j = lax.broadcasted_iota(jnp.int32, (n, n), 0)
    t = lax.broadcasted_iota(jnp.int32, (n, n), 1)
    sign = jnp.where((j + t) % 2 == 1, 1.0, -1.0)
    ahead = jnp.where(j < t, sign, 0.0)
    behind = jnp.where(j >= t, -sign, 0.0)
    weights = jnp.where(t <= n // 2, ahead, behind)
    c_row = jnp.sum(weights * g_col, axis=0, keepdims=True) / (tau * rho)
    unit = eye(n)
    s_row = jnp.sum(unit * s_col, axis=0, keepdims=True)
    h_row = jnp.sum(unit * h_col, axis=0, keepdims=True)
    u_row = jnp.sum(unit * u_col, axis=0, keepdims=True)
    t_row = lax.broadcasted_iota(jnp.int32, (1, n), 1)
    border = (t_row == 0) | (t_row == n - 1)
    a_row = jnp.where(border, 1.0, 1.0 + rho * rho)
    b_row = jnp.where(border, 0.0, 2.0 * rho * comp)
    scale = 1.0 / extent
    rows = [
        (tau * a_row * s_row - 2.0 * tau * rho * c_row) * scale,
        (tau * b_row * s_row - 2.0 * tau * comp * c_row) * scale,
        (noise * h_row + 2.0 * u_row) * scale,
    ]
    first = 2 * lax.axis_index("tm")
    two = lax.broadcasted_iota(jnp.int32, (1, 2), 1)
    for i, row in enumerate(rows):
        low = jnp.sum(jnp.where(t_row == first, row, 0.0), axis=1, keepdims=True)
        high = jnp.sum(jnp.where(t_row == first + 1, row, 0.0), axis=1, keepdims=True)
        grad_ref[pl.ds(i, 1), :] = jnp.where(two == 0, low, high)


def shaped(*shapes):
    return [jax.ShapeDtypeStruct(s, F32) for s in shapes]


def on_device(hyper_params, space_precision, data_precision, covariates, fixed_precision):
    n = 2 * lax.axis_size("tm")
    levels = n.bit_length() - 1
    half, extent = space_precision.shape
    fixed = covariates.shape[1]
    day = 2 * lax.axis_index("tm") + lax.axis_index("blk")
    tau = jnp.exp(hyper_params[0])
    rho = jnp.tanh(hyper_params[1])
    noise = jnp.exp(hyper_params[2])
    weight = jnp.where((day == 0) | (day == n - 1), 1.0, 1.0 + rho * rho)
    scalars = jnp.stack([tau, rho, noise, tau * weight])
    square = (extent, extent)
    side = (fixed, extent)
    packed = (extent + half, half)
    k, h, z, a, s0 = pl.pallas_call(
        exchange_kernel,
        out_shape=shaped(square, square, side, square, side),
        in_specs=[SMEM] + [VMEM] * 3,
        out_specs=[VMEM] * 5,
        scratch_shapes=[pltpu.SemaphoreType.DMA((3,)), pltpu.SemaphoreType.DMA((3,))],
        compiler_params=pltpu.CompilerParams(collective_id=0, has_side_effects=True),
    )(scalars, space_precision, data_precision, covariates)
    x = pl.pallas_call(
        first_kernel,
        out_shape=shaped(square)[0],
        in_specs=[VMEM],
        out_specs=VMEM,
        scratch_shapes=[pltpu.VMEM(square, F32)],
    )(a)
    return pl.pallas_call(
        functools.partial(main_kernel, levels),
        out_shape=shaped((2, half, extent), (3, 2), (fixed, fixed)),
        in_specs=[SMEM] + [VMEM] * 7,
        out_specs=[VMEM] * 3,
        scratch_shapes=[pltpu.VMEM((levels,) + packed, F32)]
        + [pltpu.VMEM((levels,) + square, F32)] * 2
        + [pltpu.VMEM((levels,) + side, F32)]
        + [pltpu.VMEM((levels,) + packed, F32)] * 2
        + [pltpu.VMEM((levels,) + square, F32)] * 2
        + [pltpu.VMEM((levels,) + side, F32)] * 2
        + [pltpu.VMEM((4,) + packed, F32)]
        + [
            pltpu.VMEM((n, fixed + 8, 4 * fixed), F32),
            pltpu.VMEM(square, F32),
            pltpu.SemaphoreType.DMA((levels, 6)),
            pltpu.SemaphoreType.DMA((levels, 6)),
            pltpu.SemaphoreType.DMA((n,)),
            pltpu.SemaphoreType.DMA((n,)),
            pltpu.SemaphoreType.DMA((2,)),
        ],
        compiler_params=pltpu.CompilerParams(
            collective_id=1, has_side_effects=True, vmem_limit_bytes=48 * 1024 * 1024
        ),
    )(scalars, k, h, z, a, s0, x, fixed_precision[None])


def solution(mesh):
    in_specs = (
        P("grp"),
        P("blk", None),
        P(("grp", "tm"), "blk", None),
        P(("grp", "tm"), None, "blk"),
        P("grp"),
    )
    out_specs = (P(("grp", "tm"), "blk", None), P(None, ("grp", "tm")), P("grp", None))
    return jax.shard_map(
        on_device, mesh=mesh, in_specs=in_specs, out_specs=out_specs, check_vma=False
    )
```

```python
import functools

import jax
import jax.numpy as jnp
from jax import lax
from jax.experimental import pallas as pl
from jax.experimental.pallas import tpu as pltpu
from jax.sharding import PartitionSpec as P

HIGHEST = lax.Precision.HIGHEST
F32 = jnp.float32
BF16 = jnp.bfloat16
VMEM = pl.BlockSpec(memory_space=pltpu.VMEM)
SMEM = pl.BlockSpec(memory_space=pltpu.SMEM)
CLOSE = 1e-6
STEPS = 40
DOUBLINGS = 5
MESH = pl.DeviceIdType.MESH


def nn(a, b):
    return three(a, b)


def nt(a, b):
    ah, al = split(a)
    bh, bl = split(b)
    return bdot_t(ah, bh) + (bdot_t(ah, bl) + bdot_t(al, bh))


def full_dot(a, b):
    return jnp.dot(a, b, precision=HIGHEST, preferred_element_type=F32)


def eye(n):
    return (
        lax.broadcasted_iota(jnp.int32, (n, n), 0) == lax.broadcasted_iota(jnp.int32, (n, n), 1)
    ).astype(F32)


def squares(r):
    return jnp.sum(r * r)


def safe_start(a):
    unit = eye(a.shape[0])
    diag_row = jnp.sum(a * unit, axis=0, keepdims=True)
    diag_col = jnp.sum(a * unit, axis=1, keepdims=True)
    scaled = jnp.abs(a) * lax.rsqrt(diag_row) * lax.rsqrt(diag_col)
    bound = jnp.max(jnp.sum(scaled, axis=0, keepdims=True))
    return unit / (diag_row * bound)


def series(x_ref, r_ref):
    def more(state):
        count, size = state
        return (count < 12) & (size > 1e-4)

    def step(state):
        count, _ = state
        r = r_ref[...].astype(BF16)
        x_ref[...] += jnp.dot(r, x_ref[...].astype(BF16), preferred_element_type=F32)
        r_new = jnp.dot(r, r, preferred_element_type=F32)
        r_ref[...] = r_new
        return count + 1, squares(r_new)

    lax.while_loop(more, step, (0, squares(r_ref[...])))


def polish(a, x_ref):
    unit = eye(a.shape[0])

    def more(state):
        count, size, before = state
        return (count < STEPS) & (size > CLOSE) & ((size < before) | (size > 0.5))

    def step(state):
        count, size, _ = state
        r = unit - full_dot(a, x_ref[...])
        new = squares(r)
        restart = (count == 0) & ~(new < 0.8)

        @pl.when(restart)
        def _():
            x_ref[...] = safe_start(a)

        @pl.when(jnp.logical_not(restart))
        def _():
            x_ref[...] += nn(x_ref[...], r)

        return count + 1, jnp.where(restart, 1e30, new), jnp.where(restart, 2e30, size)

    lax.while_loop(more, step, (0, jnp.float32(1e30), jnp.float32(2e30)))


def split(a):
    high = a.astype(BF16)
    return high, (a - high.astype(F32)).astype(BF16)


def bdot_t(a, b):
    return lax.dot_general(a, b, (((1,), (1,)), ((), ())), preferred_element_type=F32)


def bdot(a, b):
    return jnp.dot(a, b, preferred_element_type=F32)


def three(a, b):
    ah, al = split(a)
    bh, bl = split(b)
    return bdot(ah, bh) + (bdot(ah, bl) + bdot(al, bh))


def first_kernel(a_ref, x_ref, r_ref):
    a = a_ref[...]
    start = safe_start(a)
    x_ref[...] = start
    r_ref[...] = eye(a.shape[0]) - jnp.sum(start, axis=1, keepdims=True) * a
    series(x_ref, r_ref)
    polish(a, x_ref)


def exchange_kernel(c_ref, space, data, cov, k_ref, h_ref, z_ref, a_ref, s_ref, ssem, rsem):
    core = lax.axis_index("blk")
    peer = {"blk": 1 - core}
    half = space.shape[0]
    barrier = pltpu.get_barrier_semaphore()
    pl.semaphore_signal(barrier, inc=1, device_id=peer, device_id_type=MESH)
    pl.semaphore_wait(barrier, 1)
    own = pl.ds(pl.multiple_of(core * half, half), half)
    sends = [
        (space, k_ref.at[own, :]),
        (data.at[1 - core], h_ref.at[own, :]),
        (cov.at[1 - core], z_ref.at[:, own]),
    ]
    copies = [
        pltpu.make_async_remote_copy(
            src_ref=src,
            dst_ref=dst,
            send_sem=ssem.at[i],
            recv_sem=rsem.at[i],
            device_id=peer,
            device_id_type=MESH,
        )
        for i, (src, dst) in enumerate(sends)
    ]
    for copy in copies:
        copy.start()
    k_ref[own, :] = space[...]
    h_ref[own, :] = data[core]
    z_ref[:, own] = cov[core]
    for copy in copies:
        copy.wait()
    h = h_ref[...]
    a_ref[...] = c_ref[3] * k_ref[...] + c_ref[2] * h
    s_ref[...] = c_ref[2] * nn(z_ref[...], h)


def warm_inverse(a, old, delta, doublings):
    x = old
    r = three(old, delta)
    for step in range(doublings):
        rh, rl = split(r)
        xh, xl = split(x)
        x = x + (bdot(rh, xh) + (bdot(rh, xl) + bdot(rl, xh)))
        if step < doublings - 1:
            r = bdot(rh, rh) + (bdot(rh, rl) + bdot(rl, rh))
    residual = eye(a.shape[0]) - nn(a, x)
    return x + three(x, residual)


def pack(ref, x):
    n = x.shape[0]
    half = n // 2
    ref[pl.ds(0, n), :] = x[:, :half]
    ref[pl.ds(n, half), :] = x[half:, half:]


def unpack(ref):
    half = ref.shape[-1]
    left = ref[pl.ds(0, 2 * half), :]
    right = jnp.concatenate([left[half:, :].T, ref[pl.ds(2 * half, half), :]], axis=0)
    return jnp.concatenate([left, right], axis=1)


def main_kernel(levels, c_ref, k_ref, h_ref, z_ref, a_in, s0_ref, x0_ref, prior_ref, *rest):
    out_ref, grad_ref, fixed_ref = rest[:3]
    xo, lo, uo, so, xs, xr, ls, ur, ss, sr, early, all_ref, full, gtile, *sems = rest[3:]
    ssem, rsem, psend, precv, hsem = sems
    n = 1 << levels
    core = lax.axis_index("blk")
    position = lax.axis_index("tm")
    day = 2 * position + core
    half = out_ref.shape[1]
    f = s0_ref.shape[0]

    def device(t):
        return {"tm": t // 2, "blk": t % 2}

    barrier = pltpu.get_barrier_semaphore()

    @pl.loop(1, n)
    def _(o):
        pl.semaphore_signal(
            barrier, inc=1, device_id=device((day + o) % n), device_id_type=MESH
        )

    pl.semaphore_wait(barrier, n - 1)

    def transfer(src, dst, level, slot, t):
        return pltpu.make_async_remote_copy(
            src_ref=src,
            dst_ref=dst,
            send_sem=ssem.at[level, slot],
            recv_sem=rsem.at[level, slot],
            device_id=device(t),
            device_id_type=MESH,
        )

    def route(level, which):
        d = 1 << level
        if which == 0:
            src = xo.at[level]
            pair = ((src, xs.at[level]), (src, xr.at[level]))
        elif which == 1:
            src = s0_ref if level == 0 else so.at[level - 1]
            pair = ((src, ss.at[level]), (src, sr.at[level]))
        elif level == 1:
            pair = ((early.at[0], early.at[2]), (early.at[1], early.at[3]))
        else:
            pair = ((lo.at[level], ls.at[level]), (uo.at[level], ur.at[level]))
        later = transfer(*pair[0], level, 2 * which, (day + d) % n)
        earlier = transfer(*pair[1], level, 2 * which + 1, (day + n - d) % n)
        return d, later, earlier, pair[0][1], pair[1][1]

    def send(level, which):
        d, later, earlier, low, high = route(level, which)

        @pl.when(day + d < n)
        def _():
            later.start()

        @pl.when(day >= d)
        def _():
            earlier.start()

    def receive(level, which):
        d, later, earlier, low, high = route(level, which)

        @pl.when(day >= d)
        def _():
            later.wait_recv()

        @pl.when(day < d)
        def _():
            low[...] = jnp.zeros_like(low)

        @pl.when(day + d < n)
        def _():
            earlier.wait_recv()

        @pl.when(day + d >= n)
        def _():
            high[...] = jnp.zeros_like(high)

    def sent(level, which):
        d, later, earlier, low, high = route(level, which)

        @pl.when(day + d < n)
        def _():
            later.wait_send()

        @pl.when(day >= d)
        def _():
            earlier.wait_send()

    pack(xo.at[0], x0_ref[...])
    send(0, 0)
    send(0, 1)
    k = k_ref[...]
    couple = -(c_ref[0] * c_ref[1]) * k

    def gate(flag):
        return jnp.where(flag, 1.0, 0.0) * couple

    lo[0] = gate(day >= 1)
    uo[0] = gate(day <= n - 2)
    ls[0] = gate(day >= 2)
    ur[0] = gate(day <= n - 3)
    a = a_in[...]
    s = s0_ref[...]
    x = x0_ref[...]
    for level in range(levels):
        last = level == levels - 1
        receive(level, 0)
        l = lo[level]
        u = uo[level]
        p = nn(l, unpack(xs.at[level]))
        q = nn(u, unpack(xr.at[level]))
        delta = nt(p, l) + nt(q, u)
        receive(level, 1)
        s = s - nt(ss[level], p) - nt(sr[level], q)
        a = a - delta
        if not last:
            so[level] = s
            send(level + 1, 1)
            if level > 0:
                receive(level, 2)
            l_far = unpack(early.at[2]) if level == 1 else ls[level]
            u_far = unpack(early.at[3]) if level == 1 else ur[level]
            l_new = -nn(p, l_far)
            u_new = -nn(q, u_far)
            lo[level + 1] = l_new
            uo[level + 1] = u_new
            if level == 0:
                pack(early.at[0], l_new)
                pack(early.at[1], u_new)
            if level + 1 < levels - 1:
                send(level + 1, 2)
        x = warm_inverse(a, x, delta, min(DOUBLINGS, levels - level + 2))
        if not last:
            pack(xo.at[level + 1], x)
            send(level + 1, 0)

    y = nn(s, x)
    s0 = s0_ref[...]
    h = h_ref[...]
    ys = nt(y, s0)
    yky = nt(nn(y, k), y)
    yhy = nt(nn(y, h), y)
    tau, rho, noise = c_ref[0], c_ref[1], c_ref[2]
    border = (day == 0) | (day == n - 1)
    space_scale = tau * jnp.where(border, 1.0, 1.0 + rho * rho)
    s_chain = jnp.sum(jnp.sum(x * k, axis=0, keepdims=True), axis=1, keepdims=True)
    h_chain = jnp.sum(jnp.sum(x * h, axis=0, keepdims=True), axis=1, keepdims=True)
    both = jnp.concatenate(
        [nt(s0, z_ref[...]) - ys, space_scale * yky + noise * yhy - ys], axis=1
    )
    all_ref[day, pl.ds(0, f // 2), :] = jnp.concatenate([both[: f // 2], both[f // 2 :]], axis=1)
    all_ref[day, pl.ds(f // 2, 8), :] = jnp.broadcast_to(
        space_scale * s_chain + noise * h_chain, (8, 4 * f)
    )

    def packet(to, slot):
        return pltpu.make_async_remote_copy(
            src_ref=all_ref.at[day],
            dst_ref=all_ref.at[slot],
            send_sem=psend.at[to],
            recv_sem=precv.at[slot],
            device_id=device(to),
            device_id_type=MESH,
        )

    @pl.loop(1, n)
    def _(o):
        packet((day + o) % n, day).start()

    @pl.loop(1, n)
    def _(o):
        packet((day + o) % n, (day + o) % n).wait_recv()

    heads = all_ref[:, pl.ds(0, f // 2), :]
    total = jnp.sum(heads, axis=0)
    total = jnp.concatenate([total[:, :f], total[:, 2 * f : 3 * f]], axis=0)
    sigma = gauss_jordan(eye(f) * prior_ref[...] + total)
    fixed_ref[...] = sigma
    full[...] = x + lax.dot_general(
        y, nn(sigma, y), (((0,), (0,)), ((), ())), precision=HIGHEST, preferred_element_type=F32
    )
    swap = pltpu.make_async_remote_copy(
        src_ref=full.at[pl.ds(pl.multiple_of((1 - core) * half, half), half), :],
        dst_ref=out_ref.at[core],
        send_sem=hsem.at[0],
        recv_sem=hsem.at[1],
        device_id={"blk": 1 - core},
        device_id_type=MESH,
    )
    swap.start()
    blank = jnp.zeros((f // 2, f), F32)
    tiled = jnp.concatenate([blank, sigma[: f // 2], blank, sigma[f // 2 :]], axis=1)
    g_col = jnp.sum(jnp.sum(heads * tiled[None], axis=1), axis=1, keepdims=True)
    g_col = g_col + all_ref[:, pl.ds(f // 2, 8), :][:, 0, 0:1] - float(x.shape[0])

    def against(block):
        return jnp.sum(
            jnp.sum(block * sigma, axis=0, keepdims=True), axis=1, keepdims=True
        )

    grads = gradients_of(
        c_ref, g_col, s_chain + against(yky), h_chain + against(yhy), -against(ys), day, x.shape[0]
    )
    line = lax.broadcasted_iota(jnp.int32, (8, 128), 0)
    tile = jnp.where(line == 0, grads[0], jnp.where(line == 1, grads[1], grads[2]))
    gtile[core] = tile
    share = pltpu.make_async_remote_copy(
        src_ref=gtile.at[core],
        dst_ref=gtile.at[core],
        send_sem=hsem.at[2],
        recv_sem=hsem.at[3],
        device_id={"blk": 1 - core},
        device_id_type=MESH,
    )
    share.start()
    out_ref[core] = full[pl.ds(pl.multiple_of(core * half, half), half), :]

    @pl.loop(1, n)
    def _(o):
        packet((day + o) % n, day).wait_send()

    for level in range(levels):
        sent(level, 0)
        sent(level, 1)
        if 0 < level < levels - 1:
            sent(level, 2)
    share.wait()
    two = lax.broadcasted_iota(jnp.int32, (3, 2), 1)
    grad_ref[...] = jnp.where(two == 0, gtile[0, pl.ds(0, 3), 0:2], gtile[1, pl.ds(0, 3), 0:2])
    swap.wait()


def gauss_jordan(m):
    n = m.shape[0]
    rows = lax.broadcasted_iota(jnp.int32, (n, n), 0)
    cols = lax.broadcasted_iota(jnp.int32, (n, n), 1)
    for k in range(n):
        row = m[k : k + 1, :]
        col = m[:, k : k + 1]
        inv = 1.0 / m[k : k + 1, k : k + 1]
        row_s = row * inv
        m_next = m - col * row_s
        m_next = jnp.where(rows == k, row_s, m_next)
        m_next = jnp.where(cols == k, -col * inv, m_next)
        m = jnp.where((rows == k) & (cols == k), inv, m_next)
    return m


def gradients_of(c_ref, g_col, s_own, h_own, u_own, day, extent):
    n = g_col.shape[0]
    tau, rho, noise = c_ref[0], c_ref[1], c_ref[2]
    comp = 1.0 - rho * rho
    j = lax.broadcasted_iota(jnp.int32, (n, 1), 0)
    sign = jnp.where((j + day) % 2 == 1, 1.0, -1.0)
    ahead = jnp.where(j < day, sign, 0.0)
    behind = jnp.where(j >= day, -sign, 0.0)
    weights = jnp.where(day <= n // 2, ahead, behind)
    c_own = jnp.sum(weights * g_col, axis=0, keepdims=True) / (tau * rho)
    border = (day == 0) | (day == n - 1)
    a_day = jnp.where(border, 1.0, 1.0 + rho * rho)
    b_day = jnp.where(border, 0.0, 2.0 * rho * comp)
    return [
        (tau * a_day * s_own - 2.0 * tau * rho * c_own) / extent,
        (tau * b_day * s_own - 2.0 * tau * comp * c_own) / extent,
        (noise * h_own + 2.0 * u_own) / extent,
    ]


def shaped(*shapes):
    return [jax.ShapeDtypeStruct(s, F32) for s in shapes]


def on_device(hyper_params, space_precision, data_precision, covariates, fixed_precision):
    n = 2 * lax.axis_size("tm")
    levels = n.bit_length() - 1
    half, extent = space_precision.shape
    fixed = covariates.shape[1]
    day = 2 * lax.axis_index("tm") + lax.axis_index("blk")
    tau = jnp.exp(hyper_params[0])
    rho = jnp.tanh(hyper_params[1])
    noise = jnp.exp(hyper_params[2])
    weight = jnp.where((day == 0) | (day == n - 1), 1.0, 1.0 + rho * rho)
    scalars = jnp.stack([tau, rho, noise, tau * weight])
    square = (extent, extent)
    side = (fixed, extent)
    packed = (extent + half, half)
    k, h, z, a, s0 = pl.pallas_call(
        exchange_kernel,
        out_shape=shaped(square, square, side, square, side),
        in_specs=[SMEM] + [VMEM] * 3,
        out_specs=[VMEM] * 5,
        scratch_shapes=[pltpu.SemaphoreType.DMA((3,)), pltpu.SemaphoreType.DMA((3,))],
        compiler_params=pltpu.CompilerParams(collective_id=0, has_side_effects=True),
    )(scalars, space_precision, data_precision, covariates)
    x = pl.pallas_call(
        first_kernel,
        out_shape=shaped(square)[0],
        in_specs=[VMEM],
        out_specs=VMEM,
        scratch_shapes=[pltpu.VMEM(square, F32)],
    )(a)
    return pl.pallas_call(
        functools.partial(main_kernel, levels),
        out_shape=shaped((2, half, extent), (3, 2), (fixed, fixed)),
        in_specs=[SMEM] + [VMEM] * 7,
        out_specs=[VMEM] * 3,
        scratch_shapes=[pltpu.VMEM((levels,) + packed, F32)]
        + [pltpu.VMEM((levels,) + square, F32)] * 2
        + [pltpu.VMEM((levels,) + side, F32)]
        + [pltpu.VMEM((levels,) + packed, F32)] * 2
        + [pltpu.VMEM((levels,) + square, F32)] * 2
        + [pltpu.VMEM((levels,) + side, F32)] * 2
        + [pltpu.VMEM((4,) + packed, F32)]
        + [
            pltpu.VMEM((n, fixed // 2 + 8, 4 * fixed), F32),
            pltpu.VMEM(square, F32),
            pltpu.VMEM((2, 8, 128), F32),
            pltpu.SemaphoreType.DMA((levels, 6)),
            pltpu.SemaphoreType.DMA((levels, 6)),
            pltpu.SemaphoreType.DMA((n,)),
            pltpu.SemaphoreType.DMA((n,)),
            pltpu.SemaphoreType.DMA((4,)),
        ],
        compiler_params=pltpu.CompilerParams(
            collective_id=1, has_side_effects=True, vmem_limit_bytes=48 * 1024 * 1024
        ),
    )(scalars, k, h, z, a, s0, x, fixed_precision[None])


def solution(mesh):
    in_specs = (
        P("grp"),
        P("blk", None),
        P(("grp", "tm"), "blk", None),
        P(("grp", "tm"), None, "blk"),
        P("grp"),
    )
    out_specs = (P(("grp", "tm"), "blk", None), P(None, ("grp", "tm")), P("grp", None))
    return jax.shard_map(
        on_device, mesh=mesh, in_specs=in_specs, out_specs=out_specs, check_vma=False
    )
```

```python
import functools

import jax
import jax.numpy as jnp
from jax import lax
from jax.experimental import pallas as pl
from jax.experimental.pallas import tpu as pltpu
from jax.sharding import PartitionSpec as P

HIGHEST = lax.Precision.HIGHEST
F32 = jnp.float32
BF16 = jnp.bfloat16
VMEM = pl.BlockSpec(memory_space=pltpu.VMEM)
SMEM = pl.BlockSpec(memory_space=pltpu.SMEM)
CLOSE = 1e-6
STEPS = 40
DOUBLINGS = 5
MESH = pl.DeviceIdType.MESH


def nn(a, b):
    return three(a, b)


def nt(a, b):
    ah, al = split(a)
    bh, bl = split(b)
    return bdot_t(ah, bh) + (bdot_t(ah, bl) + bdot_t(al, bh))


def full_dot(a, b):
    return jnp.dot(a, b, precision=HIGHEST, preferred_element_type=F32)


def eye(n):
    return (
        lax.broadcasted_iota(jnp.int32, (n, n), 0) == lax.broadcasted_iota(jnp.int32, (n, n), 1)
    ).astype(F32)


def squares(r):
    return jnp.sum(r * r)


def safe_start(a):
    unit = eye(a.shape[0])
    diag_row = jnp.sum(a * unit, axis=0, keepdims=True)
    diag_col = jnp.sum(a * unit, axis=1, keepdims=True)
    scaled = jnp.abs(a) * lax.rsqrt(diag_row) * lax.rsqrt(diag_col)
    bound = jnp.max(jnp.sum(scaled, axis=0, keepdims=True))
    return unit / (diag_row * bound)


def series(x_ref, r_ref):
    def more(state):
        count, size = state
        return (count < 12) & (size > 1e-4)

    def step(state):
        count, _ = state
        r = r_ref[...].astype(BF16)
        x_ref[...] += jnp.dot(r, x_ref[...].astype(BF16), preferred_element_type=F32)
        r_new = jnp.dot(r, r, preferred_element_type=F32)
        r_ref[...] = r_new
        return count + 1, squares(r_new)

    lax.while_loop(more, step, (0, squares(r_ref[...])))


def polish(a, x_ref):
    unit = eye(a.shape[0])

    def more(state):
        count, size, before = state
        return (count < STEPS) & (size > CLOSE) & ((size < before) | (size > 0.5))

    def step(state):
        count, size, _ = state
        r = unit - full_dot(a, x_ref[...])
        new = squares(r)
        restart = (count == 0) & ~(new < 0.8)

        @pl.when(restart)
        def _():
            x_ref[...] = safe_start(a)

        @pl.when(jnp.logical_not(restart))
        def _():
            x_ref[...] += nn(x_ref[...], r)

        return count + 1, jnp.where(restart, 1e30, new), jnp.where(restart, 2e30, size)

    lax.while_loop(more, step, (0, jnp.float32(1e30), jnp.float32(2e30)))


def split(a):
    high = a.astype(BF16)
    return high, (a - high.astype(F32)).astype(BF16)


def bdot_t(a, b):
    return lax.dot_general(a, b, (((1,), (1,)), ((), ())), preferred_element_type=F32)


def bdot(a, b):
    return jnp.dot(a, b, preferred_element_type=F32)


def three(a, b):
    ah, al = split(a)
    bh, bl = split(b)
    return bdot(ah, bh) + (bdot(ah, bl) + bdot(al, bh))


def first_kernel(a_ref, x_ref, r_ref):
    a = a_ref[...]
    start = safe_start(a)
    x_ref[...] = start
    r_ref[...] = eye(a.shape[0]) - jnp.sum(start, axis=1, keepdims=True) * a
    series(x_ref, r_ref)
    polish(a, x_ref)


def exchange_kernel(c_ref, space, data, cov, k_ref, h_ref, z_ref, a_ref, s_ref, ssem, rsem):
    core = lax.axis_index("blk")
    peer = {"blk": 1 - core}
    half = space.shape[0]
    barrier = pltpu.get_barrier_semaphore()
    pl.semaphore_signal(barrier, inc=1, device_id=peer, device_id_type=MESH)
    pl.semaphore_wait(barrier, 1)
    own = pl.ds(pl.multiple_of(core * half, half), half)
    sends = [
        (space, k_ref.at[own, :]),
        (data.at[1 - core], h_ref.at[own, :]),
        (cov.at[1 - core], z_ref.at[:, own]),
    ]
    copies = [
        pltpu.make_async_remote_copy(
            src_ref=src,
            dst_ref=dst,
            send_sem=ssem.at[i],
            recv_sem=rsem.at[i],
            device_id=peer,
            device_id_type=MESH,
        )
        for i, (src, dst) in enumerate(sends)
    ]
    for copy in copies:
        copy.start()
    k_ref[own, :] = space[...]
    h_ref[own, :] = data[core]
    z_ref[:, own] = cov[core]
    for copy in copies:
        copy.wait()
    h = h_ref[...]
    a_ref[...] = c_ref[3] * k_ref[...] + c_ref[2] * h
    s_ref[...] = c_ref[2] * nn(z_ref[...], h)


def warm_inverse(a, old, delta, doublings):
    x = old
    r = three(old, delta)
    for step in range(doublings):
        rh, rl = split(r)
        xh, xl = split(x)
        x = x + (bdot(rh, xh) + (bdot(rh, xl) + bdot(rl, xh)))
        if step < doublings - 1:
            r = bdot(rh, rh) + (bdot(rh, rl) + bdot(rl, rh))
    residual = eye(a.shape[0]) - nn(a, x)
    return x + three(x, residual)


def pack(ref, x):
    n = x.shape[0]
    half = n // 2
    ref[pl.ds(0, n), :] = x[:, :half]
    ref[pl.ds(n, half), :] = x[half:, half:]


def unpack(ref):
    half = ref.shape[-1]
    left = ref[pl.ds(0, 2 * half), :]
    right = jnp.concatenate([left[half:, :].T, ref[pl.ds(2 * half, half), :]], axis=0)
    return jnp.concatenate([left, right], axis=1)


def main_kernel(levels, c_ref, k_ref, h_ref, z_ref, s0_ref, x0_ref, prior_ref, *rest):
    out_ref, grad_ref, fixed_ref = rest[:3]
    xo, lo, uo, so, xs, xr, ls, ur, ss, sr, early, all_ref, full, gtile, *sems = rest[3:]
    ssem, rsem, psend, precv, hsem = sems
    n = 1 << levels
    core = lax.axis_index("blk")
    position = lax.axis_index("tm")
    day = 2 * position + core
    half = out_ref.shape[1]
    f = s0_ref.shape[0]

    def device(t):
        return {"tm": t // 2, "blk": t % 2}

    barrier = pltpu.get_barrier_semaphore()

    @pl.loop(1, n)
    def _(o):
        pl.semaphore_signal(
            barrier, inc=1, device_id=device((day + o) % n), device_id_type=MESH
        )

    pl.semaphore_wait(barrier, n - 1)

    def transfer(src, dst, level, slot, t):
        return pltpu.make_async_remote_copy(
            src_ref=src,
            dst_ref=dst,
            send_sem=ssem.at[level, slot],
            recv_sem=rsem.at[level, slot],
            device_id=device(t),
            device_id_type=MESH,
        )

    def route(level, which):
        d = 1 << level
        if which == 0:
            src = xo.at[level]
            pair = ((src, xs.at[level]), (src, xr.at[level]))
        elif which == 1:
            src = s0_ref if level == 0 else so.at[level - 1]
            pair = ((src, ss.at[level]), (src, sr.at[level]))
        elif level == 1:
            pair = ((early.at[0], early.at[2]), (early.at[1], early.at[3]))
        else:
            pair = ((lo.at[level], ls.at[level]), (uo.at[level], ur.at[level]))
        later = transfer(*pair[0], level, 2 * which, (day + d) % n)
        earlier = transfer(*pair[1], level, 2 * which + 1, (day + n - d) % n)
        return d, later, earlier, pair[0][1], pair[1][1]

    def send(level, which):
        d, later, earlier, low, high = route(level, which)

        @pl.when(day + d < n)
        def _():
            later.start()

        @pl.when(day >= d)
        def _():
            earlier.start()

    def receive(level, which):
        d, later, earlier, low, high = route(level, which)

        @pl.when(day >= d)
        def _():
            later.wait_recv()

        @pl.when(day < d)
        def _():
            low[...] = jnp.zeros_like(low)

        @pl.when(day + d < n)
        def _():
            earlier.wait_recv()

        @pl.when(day + d >= n)
        def _():
            high[...] = jnp.zeros_like(high)

    def sent(level, which):
        d, later, earlier, low, high = route(level, which)

        @pl.when(day + d < n)
        def _():
            later.wait_send()

        @pl.when(day >= d)
        def _():
            earlier.wait_send()

    pack(xo.at[0], x0_ref[...])
    send(0, 0)
    send(0, 1)
    k = k_ref[...]
    couple = -(c_ref[0] * c_ref[1]) * k

    def gate(flag):
        return jnp.where(flag, 1.0, 0.0) * couple

    lo[0] = gate(day >= 1)
    uo[0] = gate(day <= n - 2)
    ls[0] = gate(day >= 2)
    ur[0] = gate(day <= n - 3)
    a = c_ref[3] * k + c_ref[2] * h_ref[...]
    s = s0_ref[...]
    x = x0_ref[...]
    for level in range(levels):
        last = level == levels - 1
        receive(level, 0)
        if 0 < level < levels - 1:
            send(level, 2)
        l = lo[level]
        u = uo[level]
        p = nn(l, unpack(xs.at[level]))
        q = nn(u, unpack(xr.at[level]))
        delta = nt(p, l) + nt(q, u)
        receive(level, 1)
        s = s - nt(ss[level], p) - nt(sr[level], q)
        a = a - delta
        if not last:
            so[level] = s
            send(level + 1, 1)
        x = warm_inverse(a, x, delta, min(DOUBLINGS, levels - level + 2))
        if not last:
            pack(xo.at[level + 1], x)
            send(level + 1, 0)
            if level > 0:
                receive(level, 2)
            l_far = unpack(early.at[2]) if level == 1 else ls[level]
            u_far = unpack(early.at[3]) if level == 1 else ur[level]
            l_new = -nn(p, l_far)
            u_new = -nn(q, u_far)
            lo[level + 1] = l_new
            uo[level + 1] = u_new
            if level == 0:
                pack(early.at[0], l_new)
                pack(early.at[1], u_new)

    y = nn(s, x)
    s0 = s0_ref[...]
    h = h_ref[...]
    ys = nt(y, s0)
    yky = nt(nn(y, k), y)
    yhy = nt(nn(y, h), y)
    tau, rho, noise = c_ref[0], c_ref[1], c_ref[2]
    border = (day == 0) | (day == n - 1)
    space_scale = tau * jnp.where(border, 1.0, 1.0 + rho * rho)
    s_chain = jnp.sum(jnp.sum(x * k, axis=0, keepdims=True), axis=1, keepdims=True)
    h_chain = jnp.sum(jnp.sum(x * h, axis=0, keepdims=True), axis=1, keepdims=True)
    both = jnp.concatenate(
        [nt(s0, z_ref[...]) - ys, space_scale * yky + noise * yhy - ys], axis=1
    )
    all_ref[day, pl.ds(0, f // 2), :] = jnp.concatenate([both[: f // 2], both[f // 2 :]], axis=1)
    all_ref[day, pl.ds(f // 2, 8), :] = jnp.broadcast_to(
        space_scale * s_chain + noise * h_chain, (8, 4 * f)
    )

    def packet(to, slot):
        return pltpu.make_async_remote_copy(
            src_ref=all_ref.at[day],
            dst_ref=all_ref.at[slot],
            send_sem=psend.at[to],
            recv_sem=precv.at[slot],
            device_id=device(to),
            device_id_type=MESH,
        )

    @pl.loop(1, n)
    def _(o):
        packet((day + o) % n, day).start()

    @pl.loop(1, n)
    def _(o):
        packet((day + o) % n, (day + o) % n).wait_recv()

    heads = all_ref[:, pl.ds(0, f // 2), :]
    total = jnp.sum(heads, axis=0)
    total = jnp.concatenate([total[:, :f], total[:, 2 * f : 3 * f]], axis=0)
    sigma = gauss_jordan(eye(f) * prior_ref[...] + total)
    fixed_ref[...] = sigma
    full[...] = x + lax.dot_general(
        y, nn(sigma, y), (((0,), (0,)), ((), ())), precision=HIGHEST, preferred_element_type=F32
    )
    swap = pltpu.make_async_remote_copy(
        src_ref=full.at[pl.ds(pl.multiple_of((1 - core) * half, half), half), :],
        dst_ref=out_ref.at[core],
        send_sem=hsem.at[0],
        recv_sem=hsem.at[1],
        device_id={"blk": 1 - core},
        device_id_type=MESH,
    )
    swap.start()
    blank = jnp.zeros((f // 2, f), F32)
    tiled = jnp.concatenate([blank, sigma[: f // 2], blank, sigma[f // 2 :]], axis=1)
    g_col = jnp.sum(jnp.sum(heads * tiled[None], axis=1), axis=1, keepdims=True)
    g_col = g_col + all_ref[:, pl.ds(f // 2, 8), :][:, 0, 0:1] - float(x.shape[0])

    def against(block):
        return jnp.sum(
            jnp.sum(block * sigma, axis=0, keepdims=True), axis=1, keepdims=True
        )

    grads = gradients_of(
        c_ref, g_col, s_chain + against(yky), h_chain + against(yhy), -against(ys), day, x.shape[0]
    )
    line = lax.broadcasted_iota(jnp.int32, (8, 128), 0)
    tile = jnp.where(line == 0, grads[0], jnp.where(line == 1, grads[1], grads[2]))
    gtile[core] = tile
    share = pltpu.make_async_remote_copy(
        src_ref=gtile.at[core],
        dst_ref=gtile.at[core],
        send_sem=hsem.at[2],
        recv_sem=hsem.at[3],
        device_id={"blk": 1 - core},
        device_id_type=MESH,
    )
    share.start()
    out_ref[core] = full[pl.ds(pl.multiple_of(core * half, half), half), :]

    @pl.loop(1, n)
    def _(o):
        packet((day + o) % n, day).wait_send()

    for level in range(levels):
        sent(level, 0)
        sent(level, 1)
        if 0 < level < levels - 1:
            sent(level, 2)
    share.wait()
    two = lax.broadcasted_iota(jnp.int32, (3, 2), 1)
    grad_ref[...] = jnp.where(two == 0, gtile[0, pl.ds(0, 3), 0:2], gtile[1, pl.ds(0, 3), 0:2])
    swap.wait()


def gauss_jordan(m):
    n = m.shape[0]
    rows = lax.broadcasted_iota(jnp.int32, (n, n), 0)
    cols = lax.broadcasted_iota(jnp.int32, (n, n), 1)
    for k in range(n):
        row = m[k : k + 1, :]
        col = m[:, k : k + 1]
        inv = 1.0 / m[k : k + 1, k : k + 1]
        row_s = row * inv
        m_next = m - col * row_s
        m_next = jnp.where(rows == k, row_s, m_next)
        m_next = jnp.where(cols == k, -col * inv, m_next)
        m = jnp.where((rows == k) & (cols == k), inv, m_next)
    return m


def gradients_of(c_ref, g_col, s_own, h_own, u_own, day, extent):
    n = g_col.shape[0]
    tau, rho, noise = c_ref[0], c_ref[1], c_ref[2]
    comp = 1.0 - rho * rho
    j = lax.broadcasted_iota(jnp.int32, (n, 1), 0)
    sign = jnp.where((j + day) % 2 == 1, 1.0, -1.0)
    ahead = jnp.where(j < day, sign, 0.0)
    behind = jnp.where(j >= day, -sign, 0.0)
    weights = jnp.where(day <= n // 2, ahead, behind)
    c_own = jnp.sum(weights * g_col, axis=0, keepdims=True) / (tau * rho)
    border = (day == 0) | (day == n - 1)
    a_day = jnp.where(border, 1.0, 1.0 + rho * rho)
    b_day = jnp.where(border, 0.0, 2.0 * rho * comp)
    return [
        (tau * a_day * s_own - 2.0 * tau * rho * c_own) / extent,
        (tau * b_day * s_own - 2.0 * tau * comp * c_own) / extent,
        (noise * h_own + 2.0 * u_own) / extent,
    ]


def shaped(*shapes):
    return [jax.ShapeDtypeStruct(s, F32) for s in shapes]


def on_device(hyper_params, space_precision, data_precision, covariates, fixed_precision):
    n = 2 * lax.axis_size("tm")
    levels = n.bit_length() - 1
    half, extent = space_precision.shape
    fixed = covariates.shape[1]
    day = 2 * lax.axis_index("tm") + lax.axis_index("blk")
    tau = jnp.exp(hyper_params[0])
    rho = jnp.tanh(hyper_params[1])
    noise = jnp.exp(hyper_params[2])
    weight = jnp.where((day == 0) | (day == n - 1), 1.0, 1.0 + rho * rho)
    scalars = jnp.stack([tau, rho, noise, tau * weight])
    square = (extent, extent)
    side = (fixed, extent)
    packed = (extent + half, half)
    k, h, z, a, s0 = pl.pallas_call(
        exchange_kernel,
        out_shape=shaped(square, square, side, square, side),
        in_specs=[SMEM] + [VMEM] * 3,
        out_specs=[VMEM] * 5,
        scratch_shapes=[pltpu.SemaphoreType.DMA((3,)), pltpu.SemaphoreType.DMA((3,))],
        compiler_params=pltpu.CompilerParams(collective_id=0, has_side_effects=True),
    )(scalars, space_precision, data_precision, covariates)
    x = pl.pallas_call(
        first_kernel,
        out_shape=shaped(square)[0],
        in_specs=[VMEM],
        out_specs=VMEM,
        scratch_shapes=[pltpu.VMEM(square, F32)],
    )(a)
    return pl.pallas_call(
        functools.partial(main_kernel, levels),
        out_shape=shaped((2, half, extent), (3, 2), (fixed, fixed)),
        in_specs=[SMEM] + [VMEM] * 6,
        out_specs=[VMEM] * 3,
        scratch_shapes=[pltpu.VMEM((levels,) + packed, F32)]
        + [pltpu.VMEM((levels,) + square, F32)] * 2
        + [pltpu.VMEM((levels,) + side, F32)]
        + [pltpu.VMEM((levels,) + packed, F32)] * 2
        + [pltpu.VMEM((levels,) + square, F32)] * 2
        + [pltpu.VMEM((levels,) + side, F32)] * 2
        + [pltpu.VMEM((4,) + packed, F32)]
        + [
            pltpu.VMEM((n, fixed // 2 + 8, 4 * fixed), F32),
            pltpu.VMEM(square, F32),
            pltpu.VMEM((2, 8, 128), F32),
            pltpu.SemaphoreType.DMA((levels, 6)),
            pltpu.SemaphoreType.DMA((levels, 6)),
            pltpu.SemaphoreType.DMA((n,)),
            pltpu.SemaphoreType.DMA((n,)),
            pltpu.SemaphoreType.DMA((4,)),
        ],
        compiler_params=pltpu.CompilerParams(
            collective_id=1, has_side_effects=True, vmem_limit_bytes=48 * 1024 * 1024
        ),
    )(scalars, k, h, z, s0, x, fixed_precision[None])


def solution(mesh):
    in_specs = (
        P("grp"),
        P("blk", None),
        P(("grp", "tm"), "blk", None),
        P(("grp", "tm"), None, "blk"),
        P("grp"),
    )
    out_specs = (P(("grp", "tm"), "blk", None), P(None, ("grp", "tm")), P("grp", None))
    return jax.shard_map(
        on_device, mesh=mesh, in_specs=in_specs, out_specs=out_specs, check_vma=False
    )
```
